128 devices in a mesh: gx: 8 (over x, core), gy: 16 (over y, z).
Axes of the slice: x: 4, y: 4, z: 4, core: 2. Of those that a mesh axis runs over, the one named last changes fastest.
Arguments:
- wave_prev: float32 [256, 1024, 512], P('gx', 'gy'), may hold values from -6 to 6
- wave_now: float32 [256, 1024, 512], P('gx', 'gy'), may hold values from -6 to 6
- courant: float32 [256, 1024, 512], P('gx', 'gy'), may hold values from 0.02 to 0.18
- traces: bfloat16 [524288, 128], P(('gx', 'gy')), may hold values from -6 to 6
- pair_owner: int32 [524288, 1], P(('gx', 'gy')), may hold values from 0 to 127; in each aligned block of 4096 rows (0 to 4095, 4096 to 8191, ...) at most 64 rows name the same one
- pair_cell: int32 [524288], P(('gx', 'gy')), may hold values from 0 to 2047
- green_tiles: bfloat16 [131072, 2048], P(('gx', 'gy')), may hold values from -0.09375 to 0.09375
Outputs:
- wave_before: float32 [256, 1024, 512], P('gx', 'gy')
- wave_after: float32 [256, 1024, 512], P('gx', 'gy')
The draws below stay inside these ranges and needn't reach their ends.
Inputs may be any that keep to these rules, and one draw needn't show every extreme that they name: `pair_owner`: within the rows of one device no owner is named by more than 64 rows, a bound that some block reaches.
All inputs are finite; a program needn't handle non-finite values.
Results may differ from the reference program's by a relative error of at most 0.00049.
Values may be sent and summed in bfloat16 or wider, within the bound.
A program may use at most 192 MiB of HBM per device.

```python
import math
import jax
import jax.numpy as jnp
import numpy as np
from jax import lax

CX = 32
CY = 64
NZ = 512
TS = 128
STEPS = 4
EROWS = 4096
SLABS = 8
NX = 256
NY = 1024
CELLS = 2048
ROWS = 524288
ROWSLAB = 65536
CAP = 64
N_GX = 8
N_GY = 16
DEVICES = 128


def place_ends(drawn, key, least, high):
    index_at = [jax.random.randint(jax.random.fold_in(key, axis), (), 0, length) for axis, length in enumerate(drawn.shape)]
    main_axis = drawn.shape.index(max(drawn.shape))
    neighbour = index_at[:main_axis] + [(index_at[main_axis] + 1) % drawn.shape[main_axis]] + index_at[main_axis + 1:]
    return drawn.at[tuple(index_at)].set(least).at[tuple(neighbour)].set(high)


def steps_of(rng, extent, pieces, smallest, largest):
    loudness = 1.0
    for dim, shards_of in pieces:
        steps = jax.random.uniform(jax.random.fold_in(jax.random.fold_in(rng, 6), dim), (shards_of,), jnp.float32, smallest / len(pieces), largest / len(pieces))
        loudness = loudness * jnp.repeat(jnp.exp(steps), extent[dim] // shards_of).reshape((-1,) + (1,) * (len(extent) - 1 - dim))
    return loudness


def routed_block(key, own, number, rows, count, top, reach, slope):
    ranking = jax.random.permutation(key, count)
    crowded, common = shares(count, rows * top, reach, slope, True), shares(count, rows * top, reach, slope, False)
    places = jnp.arange(count)

    def named(tallies, turn):
        used = int((tallies > 0).sum())
        fixed = max(1, used // 4)
        shifted = fixed + (places - fixed + turn * (used - fixed)) % max(1, count - fixed)
        return jnp.zeros((count,), jnp.int32).at[ranking[jnp.where(places < fixed, places, shifted)]].set(jnp.asarray(tallies, jnp.int32))

    tallies = jnp.where(number % 4 == 0, named(crowded, number // 4), named(common, number - number // 4 - 1))
    mixed = jax.random.permutation(jax.random.fold_in(own, 3), count)
    donor, receiver = mixed[0:count // 2 * 2:2], mixed[1:count // 2 * 2:2]
    room = jnp.minimum(tallies[donor] - 1, reach - tallies[receiver]) // 2
    room = jnp.where((donor == ranking[0]) | (receiver == ranking[0]) | (tallies[receiver] == 0), 0, jnp.maximum(room, 0))
    shifted = jax.random.randint(jax.random.fold_in(own, 4), (count // 2,), 0, 1 << 20) % (room + 1)
    tallies = tallies.at[donor].add(-shifted).at[receiver].add(shifted)
    members = jnp.searchsorted(jnp.cumsum(tallies), jnp.arange(rows * top), side="right").astype(jnp.int32)
    listing = members.reshape(top, rows).T
    listing = listing[jax.random.permutation(jax.random.fold_in(own, 1), rows)]
    turn = jax.random.randint(jax.random.fold_in(own, 2), (rows, 1), 0, top)
    return jnp.take_along_axis(listing, (jnp.arange(top)[None, :] + turn) % top, axis=1)


def shares(count, total, limit, slope, full):
    portions = [(1 << 20) // math.isqrt(grade ** slope) + 1 for grade in range(1, count + 1)]
    largest = limit if full else min(limit, max(-(-total // count), total * portions[0] // sum(portions)))
    least = 1 if total - largest >= count - 1 else 0
    given, rest = [largest] + [least] * (count - 1), total - largest - least * (count - 1)
    while rest > 0:
        free = [i for i in range(1, count) if given[i] < largest] or [i for i in range(1, count) if given[i] < limit]
        whole, remaining = sum([portions[i] for i in free]), rest
        for i in free:
            more = min(limit - given[i], max(1, remaining * portions[i] // whole), rest)
            given[i] = given[i] + more
            rest = rest - more
    return np.array(given)


def noise(rng, shape, deviation, reach, split=(), kind=jnp.bfloat16):
    array = deviation * jax.random.normal(rng, shape, jnp.float32)
    if split:
        array = array * steps_of(rng, shape, split, -0.22, 0.18)
    return jnp.clip(array, -reach, reach).astype(kind)


def setup_inputs(seed: int = 0) -> dict:
    seeds = jax.random.split(jax.random.key(seed), 8)
    wave_prev = noise(seeds[0], (NX, NY, NZ), 1.0, 6.0, ((0, 8), (1, 16)), jnp.float32)
    wave_now = noise(seeds[1], (NX, NY, NZ), 1.0, 6.0, ((0, 8), (1, 16)), jnp.float32)
    courant = jnp.clip(jnp.exp(math.log(0.18) - 2.1972246 * jax.random.uniform(seeds[2], (NX, NY, NZ), jnp.float32) ** steps_of(seeds[2], (NX, NY, NZ), ((0, 8), (1, 16)), -0.2, 0.2)), 0.02, 0.18)
    traces = noise(seeds[3], (ROWS, TS), 1.0, 6.0, ((0, 128),))
    pair_owner_keys = jax.random.split(jax.random.fold_in(seeds[4], 1), ROWS // EROWS)
    pair_owner_turns = jax.random.permutation(jax.random.fold_in(seeds[4], 3), ROWS // EROWS)
    pair_owner = jax.vmap(lambda own, number: routed_block(jax.random.fold_in(seeds[4], 2), own, number, EROWS, DEVICES, 1, CAP, 2))(pair_owner_keys, pair_owner_turns).reshape((ROWS, 1))
    pair_cell = place_ends(jax.random.randint(seeds[5], (ROWS,), 0, CELLS), jax.random.fold_in(seeds[5], 1), 0, CELLS - 1).astype(jnp.int32)
    green_tiles = noise(seeds[6], (DEVICES * SLABS * TS, STEPS * NZ), (4 * SLABS * TS) ** -0.5, 0.09375, ((0, 128),))
    return dict(wave_prev=wave_prev, wave_now=wave_now, courant=courant, traces=traces, pair_owner=pair_owner, pair_cell=pair_cell, green_tiles=green_tiles)


stencil_center = -205.0 / 72.0
stencil_side = (8.0 / 5.0, -1.0 / 5.0, 8.0 / 315.0, -1.0 / 560.0)


def laplace_padded(padded, size_first, size_second, size_depth):
    middle = padded[4:4 + size_first, 4:4 + size_second, 4:4 + size_depth]
    result = 3.0 * stencil_center * middle
    for offset in range(1, 5):
        weight = stencil_side[offset - 1]
        beside_all = padded[4 + offset:4 + offset + size_first, 4:4 + size_second, 4:4 + size_depth]
        beside_all = beside_all + padded[4 - offset:4 - offset + size_first, 4:4 + size_second, 4:4 + size_depth]
        beside_all = beside_all + padded[4:4 + size_first, 4 + offset:4 + offset + size_second, 4:4 + size_depth]
        beside_all = beside_all + padded[4:4 + size_first, 4 - offset:4 - offset + size_second, 4:4 + size_depth]
        beside_all = beside_all + padded[4:4 + size_first, 4:4 + size_second, 4 + offset:4 + offset + size_depth]
        beside_all = beside_all + padded[4:4 + size_first, 4:4 + size_second, 4 - offset:4 - offset + size_depth]
        result = result + weight * beside_all
    return result


def respond(operands):
    return jnp.dot(operands[0], operands[1], preferred_element_type=jnp.float32)


def reference(wave_prev, wave_now, courant, traces, pair_owner, pair_cell, green_tiles):
    devices = N_GX * N_GY
    window = 2 * EROWS
    target = pair_owner[:, 0].astype(jnp.int32)
    row_ids = jnp.arange(ROWS, dtype=jnp.int32)
    segment = (pair_cell.astype(jnp.int32) * SLABS + row_ids // ROWSLAB).astype(jnp.int32)
    ordering = jnp.argsort(target, stable=True)
    sorted_rows = jnp.concatenate([traces[ordering], jnp.zeros((window, TS), traces.dtype)], 0)
    sorted_segment = jnp.concatenate([segment[ordering], jnp.zeros((window,), jnp.int32)], 0).astype(jnp.int32)
    counts_per = jnp.bincount(target, length=devices).astype(jnp.int32)
    starts_per = (jnp.cumsum(counts_per) - counts_per).astype(jnp.int32)

    def collect(owner):
        begin = starts_per[owner]
        rows_here = lax.dynamic_slice_in_dim(sorted_rows, begin, window, 0).astype(jnp.float32)
        segs_here = lax.dynamic_slice_in_dim(sorted_segment, begin, window, 0)
        live = jnp.arange(window, dtype=jnp.int32) < counts_per[owner]
        rows_here = jnp.where(live[:, None], rows_here, jnp.zeros_like(rows_here))
        summed = jax.ops.segment_sum(rows_here, segs_here, num_segments=CELLS * SLABS)
        return summed.reshape(CELLS, SLABS * TS).astype(jnp.bfloat16)

    gathered = lax.map(collect, jnp.arange(devices, dtype=jnp.int32))
    tiles = green_tiles.reshape(devices, SLABS * TS, STEPS * NZ)
    previous, current = wave_prev, wave_now
    for time_step in range(STEPS):
        tile_part = tiles[:, :, time_step * NZ:(time_step + 1) * NZ]
        source = lax.map(respond, (gathered, tile_part))
        source = source.reshape(N_GX, N_GY, CX, CY, NZ).transpose(0, 2, 1, 3, 4).reshape(NX, NY, NZ)
        padded = jnp.pad(current, 4)
        following = 2.0 * current - previous + courant * laplace_padded(padded, NX, NY, NZ) + source
        previous, current = current, following
    return previous, current
```

```python
import jax
import jax.numpy as jnp
from jax import lax
from jax.experimental import pallas as pl
from jax.experimental.pallas import tpu as pltpu
from jax.sharding import PartitionSpec as P

STEPS = 4
MESH = pl.DeviceIdType.MESH
F32 = jnp.float32
BF16 = jnp.bfloat16
LANES = 128
SLOTS = 64
MSG = 72
EDGE = 4
PLANES = 4

CENTER5 = 3.0 * -205.0 / 72.0 * 5.0
SIDE5 = (8.0, -1.0, 8.0 / 63.0, -1.0 / 112.0)


def iota(shape, dim):
    return lax.broadcasted_iota(jnp.int32, shape, dim)


def pack_kernel(owner_ref, cell_ref, trace_ref, out_ref, wide, rows32, slots_v, slots_s, cells_v, sem):
    blocks = owner_ref.shape[0]
    owners = out_ref.shape[0]
    before = (iota((LANES, 2 * LANES), 0) < iota((LANES, 2 * LANES), 1)).astype(F32).astype(BF16)
    carry = jnp.zeros((owners, LANES), F32)
    cells = jnp.zeros((owners, 2 * SLOTS), F32)
    for i in range(blocks):
        own = owner_ref[i : i + 1, :]
        cell = cell_ref[i : i + 1, :]
        hot = (own == iota((owners, LANES), 0)).astype(F32)
        hot16 = hot.astype(BF16)
        seen = jnp.dot(hot16, before, preferred_element_type=F32)
        rank = jnp.sum(hot * (seen[:, :LANES] + carry), axis=0, keepdims=True)
        carry = carry + seen[:, LANES:]
        rank = rank.astype(jnp.int32)
        slots_v[i : i + 1, :] = own * SLOTS + rank
        high = ((cell // SLOTS) + 1).astype(F32)
        low = (cell % SLOTS).astype(F32)
        place = iota((2 * SLOTS, LANES), 0)
        digit = jnp.where(place < SLOTS, high, low)
        digit = jnp.where(place % SLOTS == rank, digit, 0.0).astype(BF16)
        cells = cells + lax.dot_general(
            hot16, digit, (((1,), (1,)), ((), ())), preferred_element_type=F32
        )
    cells_v[...] = cells
    copy = pltpu.make_async_copy(slots_v, slots_s, sem)
    copy.start()

    @pl.loop(0, owners)
    def _(o):
        at = pl.multiple_of(o * SLOTS, SLOTS)
        wide[pl.ds(at, SLOTS), :] = jnp.zeros((SLOTS, LANES), F32)

    rows32[...] = trace_ref[...].astype(F32)
    copy.wait()

    @pl.loop(0, blocks)
    def _(i):
        base = pl.multiple_of(i * LANES, LANES)
        for j in range(LANES):
            wide[pl.ds(slots_s[i, j], 1), :] = rows32[pl.ds(base + j, 1), :]

    @pl.loop(0, owners)
    def _(o):
        at = pl.multiple_of(o * SLOTS, SLOTS)
        out_ref[o, :SLOTS, :] = wide[pl.ds(at, SLOTS), :].astype(BF16)
        out_ref[o, SLOTS:, :] = jnp.broadcast_to(cells_v[pl.ds(o, 1), :], (MSG - SLOTS, LANES)).astype(BF16)


def pack(owner, cell, traces, owners):
    rows = traces.shape[0]
    blocks = rows // LANES
    vmem = pl.BlockSpec(memory_space=pltpu.VMEM)
    return pl.pallas_call(
        pack_kernel,
        out_shape=jax.ShapeDtypeStruct((owners, MSG, LANES), BF16),
        in_specs=[vmem] * 3,
        out_specs=vmem,
        scratch_shapes=[
            pltpu.VMEM((owners * SLOTS, LANES), F32),
            pltpu.VMEM((rows, LANES), F32),
            pltpu.VMEM((blocks, LANES), jnp.int32),
            pltpu.SMEM((blocks, LANES), jnp.int32),
            pltpu.VMEM((owners, 2 * SLOTS), F32),
            pltpu.SemaphoreType.DMA,
        ],
        compiler_params=pltpu.CompilerParams(vmem_limit_bytes=32 << 20),
    )(owner, cell, traces)


def sum_slab(rows, gath, g, sources):
    cell_count = gath.shape[1]
    lane = iota((1, LANES), 1)
    highs, spots, values = [], [], []
    for i in range(0, sources, 2):
        one = rows[g * sources + i, SLOTS:, :].astype(F32)[:1, :]
        two = rows[g * sources + i + 1, SLOTS:, :].astype(F32)[:1, :]
        high = jnp.where(lane < SLOTS, one, pltpu.roll(two, SLOTS, 1))
        low = jnp.where(lane < SLOTS, pltpu.roll(one, SLOTS, 1), two)
        highs.append(high)
        spots.append((iota((SLOTS, LANES), 0).astype(F32) == low).astype(F32).astype(BF16))
        values.append(rows[g * sources + i, :SLOTS, :])
        values.append(rows[g * sources + i + 1, :SLOTS, :])
    high = jnp.concatenate(highs, axis=1)
    spot = jnp.concatenate(spots, axis=1)
    value = jnp.concatenate(values, axis=0)
    part = 8
    for first in range(0, cell_count // SLOTS, part):
        picked = []
        for h in range(first, first + part):
            here = (high == float(h + 1)).astype(F32).astype(BF16)
            picked.append(spot * jnp.broadcast_to(here, spot.shape))
        hot = jnp.concatenate(picked, axis=0)
        total = jnp.dot(hot, value, preferred_element_type=F32)
        gath[g, first * SLOTS : (first + part) * SLOTS, :] = total.astype(BF16)


def wave_kernel(
    prev_ref, now_ref, courant_ref, rows, green_ref, before_ref, after_ref,
    first, second, speed, gath, green, inject, along, band, ysend, yrecv,
    load_sem, store_sem, send_sem, recv_sem,
):
    gx, gy = lax.axis_index("gx"), lax.axis_index("gy")
    nx, ny = lax.axis_size("gx"), lax.axis_size("gy")
    size_x, size_y, size_z = now_ref.shape
    tiles = size_z // LANES
    halves = (first, second)
    low_y = 2 * EDGE
    inner = pl.ds(low_y, size_y)
    near = (
        (gx > 0, (lax.rem(gx + nx - 1, nx), gy)),
        (gx < nx - 1, (lax.rem(gx + 1, nx), gy)),
        (gy > 0, (gx, lax.rem(gy + ny - 1, ny))),
        (gy < ny - 1, (gx, lax.rem(gy + 1, ny))),
    )

    loads = []
    for i, (source, target) in enumerate(((now_ref, first), (prev_ref, second))):
        for k in range(tiles):
            loads.append(
                pltpu.make_async_copy(
                    source.at[:, :, pl.ds(k * LANES, LANES)],
                    target.at[pl.ds(EDGE, size_x), k, inner, :],
                    load_sem.at[i * tiles + k],
                )
            )
    for k in range(tiles):
        loads.append(
            pltpu.make_async_copy(
                courant_ref.at[:, :, pl.ds(k * LANES, LANES)], speed.at[:, k], load_sem.at[2 * tiles + k]
            )
        )
    loads.append(pltpu.make_async_copy(green_ref, green, load_sem.at[3 * tiles]))
    for copy in loads:
        copy.start()

    for half in halves:
        for k in range(tiles):
            for x in (*range(EDGE), *range(size_x + EDGE, size_x + 2 * EDGE)):
                half[x, k, :, :] = jnp.zeros((size_y + 4 * EDGE, LANES), F32)

            @pl.loop(EDGE, size_x + EDGE)
            def _(x, half=half, k=k):
                half[x, k, :low_y, :] = jnp.zeros((low_y, LANES), F32)
                half[x, k, low_y + size_y :, :] = jnp.zeros((low_y, LANES), F32)

    barrier = pltpu.get_barrier_semaphore()
    for _, device in near:
        pl.semaphore_signal(barrier, inc=1, device_id=device, device_id_type=MESH)

    shape = (size_z, size_z)
    apart = jnp.abs(iota(shape, 0) - iota(shape, 1))
    weight = jnp.zeros(shape, F32)
    for k in range(1, 5):
        weight = jnp.where(apart == k, SIDE5[k - 1], weight)
    band[...] = weight.astype(BF16)

    pl.semaphore_wait(barrier, 4)

    def x_copy(half, side):
        turn = int(half is second)
        source = EDGE if side == 0 else size_x
        target = size_x + EDGE if side == 0 else 0
        return pltpu.make_async_remote_copy(
            src_ref=half.at[pl.ds(source, EDGE), :, inner, :],
            dst_ref=half.at[pl.ds(target, EDGE), :, inner, :],
            send_sem=send_sem.at[side],
            recv_sem=recv_sem.at[turn, 1 - side],
            device_id=near[side][1],
            device_id_type=MESH,
        )

    def y_copy(half, side):
        turn = int(half is second)
        return pltpu.make_async_remote_copy(
            src_ref=ysend.at[side],
            dst_ref=yrecv.at[turn, 1 - side],
            send_sem=send_sem.at[2 + side],
            recv_sem=recv_sem.at[turn, 3 - side],
            device_id=near[2 + side][1],
            device_id_type=MESH,
        )

    def send_x(half):
        for side in range(2):

            @pl.when(near[side][0])
            def _(side=side):
                x_copy(half, side).start()

    def send_y(half):
        @pl.loop(0, size_x // 2)
        def _(i):
            for k in range(tiles):
                for j in range(2):
                    at = EDGE + 2 * i + j
                    to = pl.ds(EDGE * j, EDGE)
                    ysend[0, i, k, to, :] = half[at, k, low_y : low_y + EDGE, :]
                    ysend[1, i, k, to, :] = half[at, k, low_y + size_y - EDGE : low_y + size_y, :]

        for side in range(2):

            @pl.when(near[2 + side][0])
            def _(side=side):
                y_copy(half, side).start()

    def wait_x(half):
        for side in range(2):

            @pl.when(near[side][0])
            def _(side=side):
                x_copy(half, side).wait_send()
                x_copy(half, 1 - side).wait_recv()

    def wait_y(half):
        for side in range(2):

            @pl.when(near[2 + side][0])
            def _(side=side):
                y_copy(half, side).wait_send()
                y_copy(half, 1 - side).wait_recv()

                @pl.loop(0, size_x // 2)
                def _(i):
                    for k in range(tiles):
                        for j in range(2):
                            to = low_y - EDGE if side == 0 else low_y + size_y
                            half[EDGE + 2 * i + j, k, to : to + EDGE, :] = yrecv[
                                int(half is second), side, i, k, pl.ds(EDGE * j, EDGE), :
                            ]

    def compute(now, old, t, block):
        base = block * PLANES
        rows_here = PLANES * size_y
        flat = jnp.concatenate(
            [now[pl.ds(EDGE + base, PLANES), k, inner, :].reshape(rows_here, LANES) for k in range(tiles)], axis=1
        )
        top = flat.astype(BF16)
        rest = (flat - top.astype(F32)).astype(BF16)
        part = jnp.dot(top, band[...], preferred_element_type=F32) + jnp.dot(
            rest, band[...], preferred_element_type=F32
        )
        at = pl.multiple_of(base * size_y, rows_here)
        slabs = gath.shape[0]
        left = jnp.concatenate([gath[g, pl.ds(at, rows_here), :] for g in range(slabs)], axis=1)
        source = jnp.dot(left, green[:, t * size_z : (t + 1) * size_z], preferred_element_type=F32)
        for k in range(tiles):
            lanes = slice(k * LANES, (k + 1) * LANES)
            along[:, k] = part[:, lanes].reshape(PLANES, size_y, LANES)
            inject[:, k] = source[:, lanes].reshape(PLANES, size_y, LANES)
        for k in range(tiles):
            for y in range(0, size_y, 8):
                column = [now[base + x, k, pl.ds(low_y + y, 8), :] for x in range(PLANES + 2 * EDGE)]
                for x in range(PLANES):
                    here = column[x + EDGE]
                    lap = CENTER5 * here + along[x, k, pl.ds(y, 8), :]
                    for d in range(1, EDGE + 1):
                        beside = column[x + EDGE + d] + column[x + EDGE - d]
                        beside = beside + now[base + x + EDGE, k, pl.ds(low_y + y + d, 8), :]
                        beside = beside + now[base + x + EDGE, k, pl.ds(low_y + y - d, 8), :]
                        lap = lap + SIDE5[d - 1] * beside
                    spot = (base + x + EDGE, k, pl.ds(low_y + y, 8), slice(None))
                    value = (here + here) - old[spot]
                    value = value + (0.2 * speed[base + x, k, pl.ds(y, 8), :]) * lap
                    old[spot] = value + inject[x, k, pl.ds(y, 8), :]

    for copy in loads[: 2 * tiles]:
        copy.wait()
    send_x(first)
    send_y(first)
    sources = ny
    slabs = gath.shape[0]

    @pl.loop(0, slabs)
    def _(g):
        sum_slab(rows, gath, g, sources)

    for copy in loads[2 * tiles :]:
        copy.wait()

    blocks = size_x // PLANES
    for t in range(STEPS):
        now, old = halves[t % 2], halves[1 - t % 2]
        wait_x(now)
        wait_y(now)

        @pl.loop(0, 2)
        def _(i):
            compute(now, old, t, i * (blocks - 1))

        if t + 1 < STEPS:
            send_x(old)

        @pl.loop(1, blocks - 1)
        def _(i):
            compute(now, old, t, i)

        if t + 1 < STEPS:
            send_y(old)
        if t >= STEPS - 2:
            out = (before_ref, after_ref)[t - STEPS + 2]
            for k in range(tiles):
                pltpu.make_async_copy(
                    old.at[pl.ds(EDGE, size_x), k, inner, :],
                    out.at[:, :, pl.ds(k * LANES, LANES)],
                    store_sem.at[(t - STEPS + 2) * tiles + k],
                ).start()
    for i, out in enumerate((before_ref, after_ref)):
        old = halves[1 - (STEPS - 2 + i) % 2]
        for k in range(tiles):
            pltpu.make_async_copy(
                old.at[pl.ds(EDGE, size_x), k, inner, :],
                out.at[:, :, pl.ds(k * LANES, LANES)],
                store_sem.at[i * tiles + k],
            ).wait()


def on_device(wave_prev, wave_now, courant, traces, pair_owner, pair_cell, green_tiles):
    slab_count, block_count = lax.axis_size("gx"), lax.axis_size("gy")
    owners = slab_count * block_count
    row_count = traces.shape[0]
    size_x, size_y, size_z = wave_now.shape
    tiles = size_z // LANES
    sent = pack(
        pair_owner.reshape(row_count // LANES, LANES),
        pair_cell.reshape(row_count // LANES, LANES),
        traces,
        owners,
    )
    got = lax.all_to_all(sent, ("gx", "gy"), split_axis=0, concat_axis=0, tiled=True)
    any_space = pl.BlockSpec(memory_space=pl.ANY)
    vmem = pl.BlockSpec(memory_space=pltpu.VMEM)
    padded = (size_x + 2 * EDGE, tiles, size_y + 4 * EDGE, LANES)
    face = (2, size_x // 2, tiles, 2 * EDGE, LANES)
    block = (PLANES, tiles, size_y, LANES)
    return pl.pallas_call(
        wave_kernel,
        out_shape=[jax.ShapeDtypeStruct(wave_now.shape, F32)] * 2,
        in_specs=[any_space, any_space, any_space, vmem, any_space],
        out_specs=[any_space, any_space],
        scratch_shapes=[
            pltpu.VMEM(padded, F32),
            pltpu.VMEM(padded, F32),
            pltpu.VMEM((size_x, tiles, size_y, LANES), F32),
            pltpu.VMEM((slab_count, size_x * size_y, LANES), BF16),
            pltpu.VMEM(green_tiles.shape, BF16),
            pltpu.VMEM(block, F32),
            pltpu.VMEM(block, F32),
            pltpu.VMEM((size_z, size_z), BF16),
            pltpu.VMEM(face, F32),
            pltpu.VMEM((2, *face), F32),
            pltpu.SemaphoreType.DMA((3 * tiles + 1,)),
            pltpu.SemaphoreType.DMA((2 * tiles,)),
            pltpu.SemaphoreType.DMA((4,)),
            pltpu.SemaphoreType.DMA((2, 4)),
        ],
        compiler_params=pltpu.CompilerParams(
            vmem_limit_bytes=56 << 20, collective_id=0, has_side_effects=True
        ),
    )(wave_prev, wave_now, courant, got, green_tiles)


def solution(mesh):
    return jax.shard_map(
        on_device,
        mesh=mesh,
        in_specs=(
            P("gx", "gy", None),
            P("gx", "gy", None),
            P("gx", "gy", None),
            P(("gx", "gy"), None),
            P(("gx", "gy"), None),
            P(("gx", "gy")),
            P(("gx", "gy"), None),
        ),
        out_specs=(P("gx", "gy", None), P("gx", "gy", None)),
        check_vma=False,
    )
```

```python
import jax
import jax.numpy as jnp
from jax import lax
from jax.experimental import pallas as pl
from jax.experimental.pallas import tpu as pltpu
from jax.sharding import PartitionSpec as P

STEPS = 4
MESH = pl.DeviceIdType.MESH
F32 = jnp.float32
BF16 = jnp.bfloat16
LANES = 128
SLOTS = 64
MSG = 72
EDGE = 4
PLANES = 4
THICK = 8

CENTER5 = 3.0 * -205.0 / 72.0 * 5.0
SIDE5 = (8.0, -1.0, 8.0 / 63.0, -1.0 / 112.0)


def iota(shape, dim):
    return lax.broadcasted_iota(jnp.int32, shape, dim)


def pack_kernel(owner_ref, cell_ref, trace_ref, out_ref, wide, rows32, slots_v, slots_s, cells_v, sem):
    blocks = owner_ref.shape[0]
    owners = out_ref.shape[0]
    before = (iota((LANES, 2 * LANES), 0) < iota((LANES, 2 * LANES), 1)).astype(F32).astype(BF16)
    carry = jnp.zeros((owners, LANES), F32)
    cells = jnp.zeros((owners, 2 * SLOTS), F32)
    for i in range(blocks):
        own = owner_ref[i : i + 1, :]
        cell = cell_ref[i : i + 1, :]
        hot = (own == iota((owners, LANES), 0)).astype(F32)
        hot16 = hot.astype(BF16)
        seen = jnp.dot(hot16, before, preferred_element_type=F32)
        rank = jnp.sum(hot * (seen[:, :LANES] + carry), axis=0, keepdims=True)
        carry = carry + seen[:, LANES:]
        rank = rank.astype(jnp.int32)
        slots_v[i : i + 1, :] = own * SLOTS + rank
        high = ((cell // SLOTS) + 1).astype(F32)
        low = (cell % SLOTS).astype(F32)
        place = iota((2 * SLOTS, LANES), 0)
        digit = jnp.where(place < SLOTS, high, low)
        digit = jnp.where(place % SLOTS == rank, digit, 0.0).astype(BF16)
        cells = cells + lax.dot_general(
            hot16, digit, (((1,), (1,)), ((), ())), preferred_element_type=F32
        )
    cells_v[...] = cells
    copy = pltpu.make_async_copy(slots_v, slots_s, sem)
    copy.start()

    @pl.loop(0, owners)
    def _(o):
        at = pl.multiple_of(o * SLOTS, SLOTS)
        wide[pl.ds(at, SLOTS), :] = jnp.zeros((SLOTS, LANES), F32)

    rows32[...] = trace_ref[...].astype(F32)
    copy.wait()

    @pl.loop(0, blocks)
    def _(i):
        base = pl.multiple_of(i * LANES, LANES)
        for j in range(LANES):
            wide[pl.ds(slots_s[i, j], 1), :] = rows32[pl.ds(base + j, 1), :]

    @pl.loop(0, owners)
    def _(o):
        at = pl.multiple_of(o * SLOTS, SLOTS)
        out_ref[o, :SLOTS, :] = wide[pl.ds(at, SLOTS), :].astype(BF16)
        out_ref[o, SLOTS:, :] = jnp.broadcast_to(cells_v[pl.ds(o, 1), :], (MSG - SLOTS, LANES)).astype(BF16)


def pack(owner, cell, traces, owners):
    rows = traces.shape[0]
    blocks = rows // LANES
    vmem = pl.BlockSpec(memory_space=pltpu.VMEM)
    return pl.pallas_call(
        pack_kernel,
        out_shape=jax.ShapeDtypeStruct((owners, MSG, LANES), BF16),
        in_specs=[vmem] * 3,
        out_specs=vmem,
        scratch_shapes=[
            pltpu.VMEM((owners * SLOTS, LANES), F32),
            pltpu.VMEM((rows, LANES), F32),
            pltpu.VMEM((blocks, LANES), jnp.int32),
            pltpu.SMEM((blocks, LANES), jnp.int32),
            pltpu.VMEM((owners, 2 * SLOTS), F32),
            pltpu.SemaphoreType.DMA,
        ],
        compiler_params=pltpu.CompilerParams(vmem_limit_bytes=32 << 20),
    )(owner, cell, traces)


def sum_slab(rows, gath, g, sources):
    cell_count = gath.shape[1]
    lane = iota((1, LANES), 1)
    highs, spots, values = [], [], []
    for i in range(0, sources, 2):
        one = rows[g * sources + i, SLOTS:, :].astype(F32)[:1, :]
        two = rows[g * sources + i + 1, SLOTS:, :].astype(F32)[:1, :]
        high = jnp.where(lane < SLOTS, one, pltpu.roll(two, SLOTS, 1))
        low = jnp.where(lane < SLOTS, pltpu.roll(one, SLOTS, 1), two)
        highs.append(high)
        spots.append((iota((SLOTS, LANES), 0).astype(F32) == low).astype(F32).astype(BF16))
        values.append(rows[g * sources + i, :SLOTS, :])
        values.append(rows[g * sources + i + 1, :SLOTS, :])
    high = jnp.concatenate(highs, axis=1)
    spot = jnp.concatenate(spots, axis=1)
    value = jnp.concatenate(values, axis=0)
    part = 8
    for first in range(0, cell_count // SLOTS, part):
        picked = []
        for h in range(first, first + part):
            here = (high == float(h + 1)).astype(F32).astype(BF16)
            picked.append(spot * jnp.broadcast_to(here, spot.shape))
        hot = jnp.concatenate(picked, axis=0)
        total = jnp.dot(hot, value, preferred_element_type=F32)
        gath[g, first * SLOTS : (first + part) * SLOTS, :] = total.astype(BF16)


def wave_kernel(
    prev_ref, now_ref, courant_ref, sent, green_ref, before_ref, after_ref,
    first, second, speed, rows, gath, green, band, ysend, yrecv,
    load_sem, store_sem, send_sem, recv_sem, row_send_sem, row_recv_sem,
):
    gx, gy = lax.axis_index("gx"), lax.axis_index("gy")
    nx, ny = lax.axis_size("gx"), lax.axis_size("gy")
    size_x, size_y, size_z = now_ref.shape
    tiles = size_z // LANES
    slabs = gath.shape[0]
    halves = (first, second)
    low_y = 2 * EDGE
    inner = pl.ds(low_y, size_y)
    near = (
        (gx > 0, (lax.rem(gx + nx - 1, nx), gy)),
        (gx < nx - 1, (lax.rem(gx + 1, nx), gy)),
        (gy > 0, (gx, lax.rem(gy + ny - 1, ny))),
        (gy < ny - 1, (gx, lax.rem(gy + 1, ny))),
    )

    loads = []
    for i, (source, target) in enumerate(((now_ref, first), (prev_ref, second))):
        for k in range(tiles):
            loads.append(
                pltpu.make_async_copy(
                    source.at[:, :, pl.ds(k * LANES, LANES)],
                    target.at[pl.ds(EDGE, size_x), k, inner, :],
                    load_sem.at[i * tiles + k],
                )
            )
    for k in range(tiles):
        loads.append(
            pltpu.make_async_copy(
                courant_ref.at[:, :, pl.ds(k * LANES, LANES)], speed.at[:, k], load_sem.at[2 * tiles + k]
            )
        )
    loads.append(pltpu.make_async_copy(green_ref, green, load_sem.at[3 * tiles]))
    for copy in loads:
        copy.start()

    for half in halves:
        for k in range(tiles):
            for x in (*range(EDGE), *range(size_x + EDGE, size_x + 2 * EDGE)):
                half[x, k, :, :] = jnp.zeros((size_y + 4 * EDGE, LANES), F32)

            @pl.loop(EDGE, size_x + EDGE)
            def _(x, half=half, k=k):
                half[x, k, :low_y, :] = jnp.zeros((low_y, LANES), F32)
                half[x, k, low_y + size_y :, :] = jnp.zeros((low_y, LANES), F32)

    def partner(along_x, core, step):
        chip, mine = gx // 2, lax.rem(gx, 2)
        there_x = 2 * lax.rem(chip + along_x, nx // 2) + lax.rem(mine + core, 2)
        inner_step = lax.rem(step, 4)
        outer_step = lax.rem(step // 4 + step, 4)
        there_y = 4 * lax.rem(gy // 4 + outer_step, ny // 4) + lax.rem(lax.rem(gy, 4) + inner_step, 4)
        return there_x, there_y

    barrier = pltpu.get_barrier_semaphore()
    for along_x in range(nx // 2):
        for core in range(2):

            @pl.loop(1 if along_x == core == 0 else 0, ny)
            def _(step, along_x=along_x, core=core):
                device = partner(along_x, core, step)
                pl.semaphore_signal(barrier, inc=1, device_id=device, device_id_type=MESH)

    shape = (size_z, size_z)
    apart = jnp.abs(iota(shape, 0) - iota(shape, 1))
    weight = jnp.zeros(shape, F32)
    for k in range(1, 5):
        weight = jnp.where(apart == k, SIDE5[k - 1], weight)
    band[...] = weight.astype(BF16)

    pl.semaphore_wait(barrier, nx * ny - 1)

    me = gx * ny + gy
    keep = pltpu.make_async_copy(sent.at[me], rows.at[me], row_recv_sem.at[gx])

    def send_rows(group):
        @pl.loop(0, ny)
        def _(step):
            for along_x in group:
                for core in range(2):

                    def send(along_x=along_x, core=core):
                        there_x, there_y = partner(along_x, core, step)
                        pltpu.make_async_remote_copy(
                            src_ref=sent.at[there_x * ny + there_y],
                            dst_ref=rows.at[me],
                            send_sem=row_send_sem,
                            recv_sem=row_recv_sem.at[gx],
                            device_id=(there_x, there_y),
                            device_id_type=MESH,
                        ).start()

                    if along_x == core == 0:
                        pl.when(step > 0)(send)
                        pl.when(step == 0)(keep.start)
                    else:
                        send()

    def wait_slab(g):
        part = rows.at[pl.ds(g * ny, ny)]
        pltpu.make_async_copy(part, part, row_recv_sem.at[g]).wait()

    def x_copy(half, side):
        source = EDGE if side == 0 else size_x
        target = size_x + EDGE if side == 0 else 0
        return pltpu.make_async_remote_copy(
            src_ref=half.at[pl.ds(source, EDGE), :, inner, :],
            dst_ref=half.at[pl.ds(target, EDGE), :, inner, :],
            send_sem=send_sem.at[side],
            recv_sem=recv_sem.at[int(half is second), 1 - side],
            device_id=near[side][1],
            device_id_type=MESH,
        )

    def y_copy(half, side):
        return pltpu.make_async_remote_copy(
            src_ref=ysend.at[side],
            dst_ref=yrecv.at[int(half is second), 1 - side],
            send_sem=send_sem.at[2 + side],
            recv_sem=recv_sem.at[int(half is second), 3 - side],
            device_id=near[2 + side][1],
            device_id_type=MESH,
        )

    def send_x(half):
        for side in range(2):

            @pl.when(near[side][0])
            def _(side=side):
                x_copy(half, side).start()

    def send_y(half):
        @pl.loop(0, size_x // 2)
        def _(i):
            for k in range(tiles):
                for j in range(2):
                    at = EDGE + 2 * i + j
                    to = pl.ds(EDGE * j, EDGE)
                    ysend[0, i, k, to, :] = half[at, k, low_y : low_y + EDGE, :]
                    ysend[1, i, k, to, :] = half[at, k, low_y + size_y - EDGE : low_y + size_y, :]

        for side in range(2):

            @pl.when(near[2 + side][0])
            def _(side=side):
                y_copy(half, side).start()

    def wait_x(half):
        for side in range(2):

            @pl.when(near[side][0])
            def _(side=side):
                x_copy(half, side).wait_send()
                x_copy(half, 1 - side).wait_recv()

    def wait_y(half):
        for side in range(2):

            @pl.when(near[2 + side][0])
            def _(side=side):
                y_copy(half, side).wait_send()
                y_copy(half, 1 - side).wait_recv()

                @pl.loop(0, size_x // 2)
                def _(i):
                    for k in range(tiles):
                        for j in range(2):
                            to = low_y - EDGE if side == 0 else low_y + size_y
                            half[EDGE + 2 * i + j, k, to : to + EDGE, :] = yrecv[
                                int(half is second), side, i, k, pl.ds(EDGE * j, EDGE), :
                            ]

    def source_of(t, base):
        at = pl.multiple_of(base * size_y, THICK * size_y)
        left = jnp.concatenate([gath[g, pl.ds(at, THICK * size_y), :] for g in range(slabs)], axis=1)
        return jnp.dot(left, green[:, t * size_z : (t + 1) * size_z], preferred_element_type=F32)

    def local_part(now, old, t, base):
        count = THICK * size_y
        place = pl.ds(EDGE + base, THICK)
        flat = jnp.concatenate([now[place, k, inner, :].reshape(count, LANES) for k in range(tiles)], axis=1)
        top = flat.astype(BF16)
        rest = (flat - top.astype(F32)).astype(BF16)
        lap = jnp.dot(top, band[...], preferred_element_type=F32)
        lap = lap + jnp.dot(rest, band[...], preferred_element_type=F32)
        source = source_of(t, base) if t else None
        for k in range(tiles):
            lanes = slice(k * LANES, (k + 1) * LANES)
            here = flat[:, lanes]
            value = (0.2 * speed[pl.ds(base, THICK), k].reshape(count, LANES)) * (CENTER5 * here + lap[:, lanes])
            value = value + (here + here) - old[place, k, inner, :].reshape(count, LANES)
            if t:
                value = value + source[:, lanes]
            old[place, k, inner, :] = value.reshape(THICK, size_y, LANES)

    def add_source(old, t, base):
        place = pl.ds(EDGE + base, THICK)
        source = source_of(t, base)
        for k in range(tiles):
            lanes = source[:, k * LANES : (k + 1) * LANES].reshape(THICK, size_y, LANES)
            old[place, k, inner, :] = old[place, k, inner, :] + lanes

    def side_part(now, old, base, ys):
        for k in range(tiles):
            for y in ys:
                column = [now[base + x, k, pl.ds(low_y + y, 8), :] for x in range(PLANES + 2 * EDGE)]
                for x in range(PLANES):
                    lap = None
                    for d in range(1, EDGE + 1):
                        beside = column[x + EDGE + d] + column[x + EDGE - d]
                        beside = beside + now[base + x + EDGE, k, pl.ds(low_y + y + d, 8), :]
                        beside = beside + now[base + x + EDGE, k, pl.ds(low_y + y - d, 8), :]
                        beside = SIDE5[d - 1] * beside
                        lap = beside if lap is None else lap + beside
                    spot = (base + x + EDGE, k, pl.ds(low_y + y, 8), slice(None))
                    old[spot] = old[spot] + (0.2 * speed[base + x, k, pl.ds(y, 8), :]) * lap

    blocks = size_x // PLANES
    thick_blocks = size_x // THICK
    every = tuple(range(0, size_y, 8))

    for copy in loads[:tiles]:
        copy.wait()
    send_rows((0, nx // 4))
    send_x(first)
    send_y(first)
    send_rows((1, nx // 2 - 1))
    for copy in loads[tiles : 3 * tiles]:
        copy.wait()

    @pl.loop(0, thick_blocks)
    def _(i):
        local_part(first, second, 0, i * THICK)

    def take_slab(along_x, core):
        g = 2 * lax.rem(gx // 2 + along_x, nx // 2) + core
        wait_slab(g)
        sum_slab(rows, gath, g, ny)

    @pl.loop(0, slabs // 2)
    def _(i):
        take_slab(lax.rem(i, 2) * (nx // 4), i // 2)

    wait_x(first)
    wait_y(first)

    @pl.loop(0, blocks)
    def _(i):
        side_part(first, second, i * PLANES, every)

    loads[3 * tiles].wait()

    @pl.loop(0, slabs // 2)
    def _(i):
        take_slab(lax.rem(i, 2) * (nx // 4) + 1, i // 2)

    most = rows.at[pl.ds(0, nx * ny - 1)]
    pltpu.make_async_copy(most, most, row_send_sem).wait()

    @pl.loop(0, 2)
    def _(i):
        add_source(second, 0, i * (size_x - THICK))

    send_x(second)

    @pl.loop(1, thick_blocks - 1)
    def _(i):
        add_source(second, 0, i * THICK)

    send_y(second)

    for t in range(1, STEPS):
        now, old = halves[t % 2], halves[1 - t % 2]

        @pl.loop(0, thick_blocks)
        def _(i):
            local_part(now, old, t, i * THICK)

        @pl.loop(1, blocks - 1)
        def _(i):
            side_part(now, old, i * PLANES, every[1:-1])

        wait_x(now)
        wait_y(now)

        @pl.loop(0, 2)
        def _(i):
            side_part(now, old, i * (size_x - PLANES), every)

        if t + 1 < STEPS:
            send_x(old)

        @pl.loop(1, blocks - 1)
        def _(i):
            side_part(now, old, i * PLANES, (every[0], every[-1]))

        if t + 1 < STEPS:
            send_y(old)
        if t >= STEPS - 2:
            out = (before_ref, after_ref)[t - STEPS + 2]
            for k in range(tiles):
                pltpu.make_async_copy(
                    old.at[pl.ds(EDGE, size_x), k, inner, :],
                    out.at[:, :, pl.ds(k * LANES, LANES)],
                    store_sem.at[(t - STEPS + 2) * tiles + k],
                ).start()
    for i, out in enumerate((before_ref, after_ref)):
        old = halves[1 - (STEPS - 2 + i) % 2]
        for k in range(tiles):
            pltpu.make_async_copy(
                old.at[pl.ds(EDGE, size_x), k, inner, :],
                out.at[:, :, pl.ds(k * LANES, LANES)],
                store_sem.at[i * tiles + k],
            ).wait()


def on_device(wave_prev, wave_now, courant, traces, pair_owner, pair_cell, green_tiles):
    slab_count, block_count = lax.axis_size("gx"), lax.axis_size("gy")
    owners = slab_count * block_count
    row_count = traces.shape[0]
    size_x, size_y, size_z = wave_now.shape
    tiles = size_z // LANES
    sent = pack(
        pair_owner.reshape(row_count // LANES, LANES),
        pair_cell.reshape(row_count // LANES, LANES),
        traces,
        owners,
    )
    any_space = pl.BlockSpec(memory_space=pl.ANY)
    padded = (size_x + 2 * EDGE, tiles, size_y + 4 * EDGE, LANES)
    face = (2, size_x // 2, tiles, 2 * EDGE, LANES)
    return pl.pallas_call(
        wave_kernel,
        out_shape=[jax.ShapeDtypeStruct(wave_now.shape, F32)] * 2,
        in_specs=[any_space] * 5,
        out_specs=[any_space, any_space],
        scratch_shapes=[
            pltpu.VMEM(padded, F32),
            pltpu.VMEM(padded, F32),
            pltpu.VMEM((size_x, tiles, size_y, LANES), F32),
            pltpu.VMEM((owners, MSG, LANES), BF16),
            pltpu.VMEM((slab_count, size_x * size_y, LANES), BF16),
            pltpu.VMEM(green_tiles.shape, BF16),
            pltpu.VMEM((size_z, size_z), BF16),
            pltpu.VMEM(face, F32),
            pltpu.VMEM((2, *face), F32),
            pltpu.SemaphoreType.DMA((3 * tiles + 1,)),
            pltpu.SemaphoreType.DMA((2 * tiles,)),
            pltpu.SemaphoreType.DMA((4,)),
            pltpu.SemaphoreType.DMA((2, 4)),
            pltpu.SemaphoreType.DMA,
            pltpu.SemaphoreType.DMA((slab_count,)),
        ],
        compiler_params=pltpu.CompilerParams(
            vmem_limit_bytes=56 << 20, collective_id=0, has_side_effects=True
        ),
    )(wave_prev, wave_now, courant, sent, green_tiles)


def solution(mesh):
    return jax.shard_map(
        on_device,
        mesh=mesh,
        in_specs=(
            P("gx", "gy", None),
            P("gx", "gy", None),
            P("gx", "gy", None),
            P(("gx", "gy"), None),
            P(("gx", "gy"), None),
            P(("gx", "gy")),
            P(("gx", "gy"), None),
        ),
        out_specs=(P("gx", "gy", None), P("gx", "gy", None)),
        check_vma=False,
    )
```

```python
import jax
import jax.numpy as jnp
from jax import lax
from jax.experimental import pallas as pl
from jax.experimental.pallas import tpu as pltpu
from jax.sharding import PartitionSpec as P

STEPS = 4
MESH = pl.DeviceIdType.MESH
F32 = jnp.float32
BF16 = jnp.bfloat16
LANES = 128
SLOTS = 64
EDGE = 4
PLANES = 2
THICK = 8

CENTER5 = 3.0 * -205.0 / 72.0 * 5.0
SIDE5 = (8.0, -1.0, 8.0 / 63.0, -1.0 / 112.0)


def iota(shape, dim):
    return lax.broadcasted_iota(jnp.int32, shape, dim)


def pack_kernel(
    owner_hbm, cell_hbm, trace_hbm, out_ref, out_cells,
    owner_ref, cell_ref, trace_ref, wide, rows32, slots_v, slots_s, cells_v, sem, load_sem,
):
    loads = [
        pltpu.make_async_copy(source, target, load_sem.at[i])
        for i, (source, target) in enumerate(
            ((owner_hbm, owner_ref), (cell_hbm, cell_ref), (trace_hbm, trace_ref))
        )
    ]
    for load in loads:
        load.start()
    blocks = owner_ref.shape[0]
    owners = out_ref.shape[0]
    before = (iota((LANES, 2 * LANES), 0) < iota((LANES, 2 * LANES), 1)).astype(F32).astype(BF16)
    carry = jnp.zeros((owners, LANES), F32)
    loads[0].wait()
    loads[1].wait()
    cells = jnp.zeros((owners, 2 * SLOTS), F32)
    for i in range(blocks):
        own = owner_ref[i : i + 1, :]
        cell = cell_ref[i : i + 1, :]
        hot = (own == iota((owners, LANES), 0)).astype(F32)
        hot16 = hot.astype(BF16)
        seen = jnp.dot(hot16, before, preferred_element_type=F32)
        rank = jnp.sum(hot * (seen[:, :LANES] + carry), axis=0, keepdims=True)
        carry = carry + seen[:, LANES:]
        rank = rank.astype(jnp.int32)
        slots_v[i : i + 1, :] = own * SLOTS + rank
        high = ((cell // SLOTS) + 1).astype(F32)
        low = (cell % SLOTS).astype(F32)
        place = iota((2 * SLOTS, LANES), 0)
        digit = jnp.where(place < SLOTS, high, low)
        digit = jnp.where(place % SLOTS == rank, digit, 0.0).astype(BF16)
        cells = cells + lax.dot_general(
            hot16, digit, (((1,), (1,)), ((), ())), preferred_element_type=F32
        )
    cells_v[...] = cells
    copy = pltpu.make_async_copy(slots_v, slots_s, sem)
    copy.start()

    @pl.loop(0, owners)
    def _(o):
        at = pl.multiple_of(o * SLOTS, SLOTS)
        wide[pl.ds(at, SLOTS), :] = jnp.zeros((SLOTS, LANES), F32)

    loads[2].wait()
    rows32[...] = trace_ref[...].astype(F32)
    copy.wait()

    @pl.loop(0, blocks)
    def _(i):
        base = pl.multiple_of(i * LANES, LANES)
        for j in range(LANES):
            wide[pl.ds(slots_s[i, j], 1), :] = rows32[pl.ds(base + j, 1), :]

    @pl.loop(0, owners)
    def _(o):
        at = pl.multiple_of(o * SLOTS, SLOTS)
        out_ref[o] = wide[pl.ds(at, SLOTS), :].astype(BF16)
        out_cells[o] = cells_v[pl.ds(o, 1), :]


def pack(owner, cell, traces, owners):
    rows = traces.shape[0]
    blocks = rows // LANES
    vmem = pl.BlockSpec(memory_space=pltpu.VMEM)
    return pl.pallas_call(
        pack_kernel,
        out_shape=(
            jax.ShapeDtypeStruct((owners, SLOTS, LANES), BF16),
            jax.ShapeDtypeStruct((owners, 1, LANES), F32),
        ),
        in_specs=[pl.BlockSpec(memory_space=pltpu.HBM)] * 3,
        out_specs=(vmem, vmem),
        scratch_shapes=[
            pltpu.VMEM((blocks, LANES), jnp.int32),
            pltpu.VMEM((blocks, LANES), jnp.int32),
            pltpu.VMEM((rows, LANES), BF16),
            pltpu.VMEM((owners * SLOTS, LANES), F32),
            pltpu.VMEM((rows, LANES), F32),
            pltpu.VMEM((blocks, LANES), jnp.int32),
            pltpu.SMEM((blocks, LANES), jnp.int32),
            pltpu.VMEM((owners, 2 * SLOTS), F32),
            pltpu.SemaphoreType.DMA,
            pltpu.SemaphoreType.DMA((3,)),
        ],
        compiler_params=pltpu.CompilerParams(vmem_limit_bytes=32 << 20),
    )(owner, cell, traces)


def sum_slab(rows, cells, gath, g, to, sources):
    cell_count = gath.shape[1]
    lane = iota((1, LANES), 1)
    highs, spots, values = [], [], []
    for i in range(0, sources, 2):
        one = cells[g * sources + i]
        two = cells[g * sources + i + 1]
        high = jnp.where(lane < SLOTS, one, pltpu.roll(two, SLOTS, 1))
        low = jnp.where(lane < SLOTS, pltpu.roll(one, SLOTS, 1), two)
        highs.append(high)
        spots.append((iota((SLOTS, LANES), 0).astype(F32) == low).astype(F32).astype(BF16))
        values.append(rows[g * sources + i])
        values.append(rows[g * sources + i + 1])
    high = jnp.concatenate(highs, axis=1)
    spot = jnp.concatenate(spots, axis=1)
    value = jnp.concatenate(values, axis=0)
    part = 8
    for first in range(0, cell_count // SLOTS, part):
        picked = []
        for h in range(first, first + part):
            here = (high == float(h + 1)).astype(F32).astype(BF16)
            picked.append(spot * jnp.broadcast_to(here, spot.shape))
        hot = jnp.concatenate(picked, axis=0)
        total = jnp.dot(hot, value, preferred_element_type=F32)
        gath[to, first * SLOTS : (first + part) * SLOTS, :] = total.astype(BF16)


def wave_kernel(
    prev_ref, now_ref, courant_ref, sent, sent_cells, green_ref, before_ref, after_ref,
    first, second, speed, rows, cells, gath, green, later, band, ysend, yrecv,
    load_sem, store_sem, send_sem, recv_sem, row_send_sem, row_recv_sem, cell_send_sem, cell_recv_sem,
):
    gx, gy = lax.axis_index("gx"), lax.axis_index("gy")
    nx, ny = lax.axis_size("gx"), lax.axis_size("gy")
    size_x, size_y, size_z = now_ref.shape
    tiles = size_z // LANES
    groups = gath.shape[0] // 2
    halves = (first, second)
    low_y = 2 * EDGE
    inner = pl.ds(low_y, size_y)
    near = (
        (gx > 0, (lax.rem(gx + nx - 1, nx), gy)),
        (gx < nx - 1, (lax.rem(gx + 1, nx), gy)),
        (gy > 0, (gx, lax.rem(gy + ny - 1, ny))),
        (gy < ny - 1, (gx, lax.rem(gy + 1, ny))),
    )

    loads = []
    for i, (source, target) in enumerate(((now_ref, first), (prev_ref, second))):
        for k in range(tiles):
            loads.append(
                pltpu.make_async_copy(
                    source.at[:, :, pl.ds(k * LANES, LANES)],
                    target.at[pl.ds(EDGE, size_x), k, inner, :],
                    load_sem.at[i * tiles + k],
                )
            )
    for k in range(tiles):
        loads.append(
            pltpu.make_async_copy(
                courant_ref.at[:, :, pl.ds(k * LANES, LANES)], speed.at[:, k], load_sem.at[2 * tiles + k]
            )
        )
    loads.append(pltpu.make_async_copy(green_ref, green, load_sem.at[3 * tiles]))
    for copy in loads:
        copy.start()

    for half in halves:
        for k in range(tiles):
            for x in (*range(EDGE), *range(size_x + EDGE, size_x + 2 * EDGE)):
                half[x, k, :, :] = jnp.zeros((size_y + 4 * EDGE, LANES), F32)

            @pl.loop(EDGE, size_x + EDGE)
            def _(x, half=half, k=k):
                half[x, k, :low_y, :] = jnp.zeros((low_y, LANES), F32)
                half[x, k, low_y + size_y :, :] = jnp.zeros((low_y, LANES), F32)

    chips, depth = nx // 2, 4

    def there_x(along, core):
        return 2 * lax.rem(gx // 2 + along, chips) + lax.rem(gx + core, 2)

    there_zs = [lax.rem(lax.rem(gy, depth) + along, depth) for along in range(depth)]

    def there_y(step, along):
        return depth * lax.rem(gy // depth + step + along, ny // depth) + there_zs[along]

    barrier = pltpu.get_barrier_semaphore()

    @pl.loop(0, ny // depth)
    def _(step):
        for along in range(depth):
            y = there_y(step, along)
            for along_x in range(chips):
                for core in range(2):
                    device = (there_x(along_x, core), y)

                    def greet(device=device):
                        pl.semaphore_signal(barrier, inc=1, device_id=device, device_id_type=MESH)

                    if along == along_x == core == 0:
                        pl.when(step > 0)(greet)
                    else:
                        greet()

    shape = (size_z, size_z)
    apart = jnp.abs(iota(shape, 0) - iota(shape, 1))
    weight = jnp.zeros(shape, F32)
    for k in range(1, 5):
        weight = jnp.where(apart == k, SIDE5[k - 1], weight)
    band[...] = weight.astype(BF16)

    pl.semaphore_wait(barrier, nx * ny - 1)

    me = gx * ny + gy
    keep = (
        pltpu.make_async_copy(sent.at[me], rows.at[me], row_recv_sem.at[gx]),
        pltpu.make_async_copy(sent_cells.at[me], cells.at[me], cell_recv_sem.at[gx]),
    )

    def send_rows(first_chip, core):
        @pl.loop(0, ny // depth)
        def _(step):
            for along in range(depth):
                y = there_y(step, along)
                for along_x in (first_chip, first_chip + chips // 2):

                    def send(x=there_x(along_x, core), y=y):
                        there = x * ny + y
                        for source, target, out_sem, in_sem in (
                            (sent_cells, cells, cell_send_sem, cell_recv_sem),
                            (sent, rows, row_send_sem, row_recv_sem),
                        ):
                            pltpu.make_async_remote_copy(
                                src_ref=source.at[there],
                                dst_ref=target.at[me],
                                send_sem=out_sem,
                                recv_sem=in_sem.at[gx],
                                device_id=(x, y),
                                device_id_type=MESH,
                            ).start()

                    if along == along_x == 0 and isinstance(core, int) and core == 0:
                        pl.when(step > 0)(send)

                        @pl.when(step == 0)
                        def _():
                            for copy in keep:
                                copy.start()

                    else:
                        send()

    def slab_of(group, which):
        chip = lax.rem(gx // 2 + group // 2 + which * (nx // 4), nx // 2)
        return 2 * chip + lax.rem(gx + group, 2)

    def wait_slabs(group):
        for which in range(2):
            g = slab_of(group, which)
            for target, in_sem in ((cells, cell_recv_sem), (rows, row_recv_sem)):
                part = target.at[pl.ds(g * ny, ny)]
                pltpu.make_async_copy(part, part, in_sem.at[g]).wait()

    def sum_slabs(group):
        @pl.loop(0, 2)
        def _(which):
            sum_slab(rows, cells, gath, slab_of(group, which), 2 * group + which, ny)

    def x_copy(half, side):
        source = EDGE if side == 0 else size_x
        target = size_x + EDGE if side == 0 else 0
        return pltpu.make_async_remote_copy(
            src_ref=half.at[pl.ds(source, EDGE), :, inner, :],
            dst_ref=half.at[pl.ds(target, EDGE), :, inner, :],
            send_sem=send_sem.at[side],
            recv_sem=recv_sem.at[int(half is second), 1 - side],
            device_id=near[side][1],
            device_id_type=MESH,
        )

    def y_copy(half, side):
        return pltpu.make_async_remote_copy(
            src_ref=ysend.at[side],
            dst_ref=yrecv.at[int(half is second), 1 - side],
            send_sem=send_sem.at[2 + side],
            recv_sem=recv_sem.at[int(half is second), 3 - side],
            device_id=near[2 + side][1],
            device_id_type=MESH,
        )

    def send_x(half):
        for side in range(2):

            @pl.when(near[side][0])
            def _(side=side):
                x_copy(half, side).start()

    def send_y(half):
        @pl.loop(0, size_x // 2)
        def _(i):
            for k in range(tiles):
                for j in range(2):
                    at = EDGE + 2 * i + j
                    to = pl.ds(EDGE * j, EDGE)
                    ysend[0, i, k, to, :] = half[at, k, low_y : low_y + EDGE, :]
                    ysend[1, i, k, to, :] = half[at, k, low_y + size_y - EDGE : low_y + size_y, :]

        for side in range(2):

            @pl.when(near[2 + side][0])
            def _(side=side):
                y_copy(half, side).start()

    def wait_x(half):
        for side in range(2):

            @pl.when(near[side][0])
            def _(side=side):
                x_copy(half, side).wait_send()
                x_copy(half, 1 - side).wait_recv()

    def wait_y(half):
        for side in range(2):

            @pl.when(near[2 + side][0])
            def _(side=side):
                y_copy(half, side).wait_send()
                y_copy(half, 1 - side).wait_recv()

                @pl.loop(0, size_x // 2)
                def _(i):
                    for k in range(tiles):
                        for j in range(2):
                            to = low_y - EDGE if side == 0 else low_y + size_y
                            half[EDGE + 2 * i + j, k, to : to + EDGE, :] = yrecv[
                                int(half is second), side, i, k, pl.ds(EDGE * j, EDGE), :
                            ]

    def source_of(half, t, base):
        at = pl.multiple_of(base * size_y, THICK * size_y)
        left, right = [], []
        for group in (2 * half, 2 * half + 1):
            for which in range(2):
                left.append(gath[2 * group + which, pl.ds(at, THICK * size_y), :])
                row = pl.multiple_of(slab_of(group, which) * LANES, LANES)
                right.append(green[pl.ds(row, LANES), t * size_z : (t + 1) * size_z])
        return jnp.dot(
            jnp.concatenate(left, axis=1), jnp.concatenate(right, axis=0), preferred_element_type=F32
        )

    def local_part(now, old, t, base):
        count = THICK * size_y
        place = pl.ds(EDGE + base, THICK)
        flat = jnp.concatenate([now[place, k, inner, :].reshape(count, LANES) for k in range(tiles)], axis=1)
        top = flat.astype(BF16)
        rest = (flat - top.astype(F32)).astype(BF16)
        lap = jnp.dot(top, band[...], preferred_element_type=F32)
        lap = lap + jnp.dot(rest, band[...], preferred_element_type=F32)
        source = source_of(1, t, base) if t else None
        for k in range(tiles):
            lanes = slice(k * LANES, (k + 1) * LANES)
            here = flat[:, lanes]
            value = (0.2 * speed[pl.ds(base, THICK), k].reshape(count, LANES)) * (CENTER5 * here + lap[:, lanes])
            value = value + (here + here) - old[place, k, inner, :].reshape(count, LANES)
            if t:
                value = value + source[:, lanes] + later[t - 1, pl.ds(base, THICK), k].reshape(count, LANES)
            old[place, k, inner, :] = value.reshape(THICK, size_y, LANES)

    def add_source(half, t, base):
        source = source_of(half, t, base)
        for k in range(tiles):
            lanes = source[:, k * LANES : (k + 1) * LANES].reshape(THICK, size_y, LANES)
            if t:
                later[t - 1, pl.ds(base, THICK), k] = lanes
            else:
                spot = (pl.ds(EDGE + base, THICK), k, inner, slice(None))
                second[spot] = second[spot] + lanes

    def side_part(now, old, base, ys):
        for k in range(tiles):
            for y in ys:
                column = [now[base + x, k, pl.ds(low_y + y, 8), :] for x in range(PLANES + 2 * EDGE)]
                for x in range(PLANES):
                    lap = None
                    for d in range(1, EDGE + 1):
                        beside = column[x + EDGE + d] + column[x + EDGE - d]
                        beside = beside + now[base + x + EDGE, k, pl.ds(low_y + y + d, 8), :]
                        beside = beside + now[base + x + EDGE, k, pl.ds(low_y + y - d, 8), :]
                        beside = SIDE5[d - 1] * beside
                        lap = beside if lap is None else lap + beside
                    spot = (base + x + EDGE, k, pl.ds(low_y + y, 8), slice(None))
                    old[spot] = old[spot] + (0.2 * speed[base + x, k, pl.ds(y, 8), :]) * lap

    blocks = size_x // PLANES
    thick_blocks = size_x // THICK
    edge_blocks = EDGE // PLANES
    every = tuple(range(0, size_y, 8))

    send_rows(0, 0)
    for copy in loads[:tiles]:
        copy.wait()
    send_x(first)
    send_y(first)
    for copy in loads[tiles : 3 * tiles]:
        copy.wait()

    @pl.loop(0, thick_blocks)
    def _(i):
        local_part(first, second, 0, i * THICK)

    send_rows(0, 1)
    wait_x(first)
    wait_y(first)

    @pl.loop(0, blocks)
    def _(i):
        side_part(first, second, i * PLANES, every)

    @pl.loop(0, 2)
    def _(group):
        wait_slabs(group)
        send_rows(1, group)
        sum_slabs(group)

    loads[3 * tiles].wait()
    for t in range(STEPS):

        @pl.loop(0, thick_blocks)
        def _(i, t=t):
            add_source(0, t, i * THICK)

    @pl.loop(2, groups)
    def _(group):
        wait_slabs(group)
        sum_slabs(group)

    for target, out_sem in ((cells, cell_send_sem), (rows, row_send_sem)):
        most = target.at[pl.ds(0, nx * ny - 1)]
        pltpu.make_async_copy(most, most, out_sem).wait()

    @pl.loop(0, thick_blocks)
    def _(i):
        add_source(1, 0, i * THICK)

    send_x(second)
    send_y(second)

    stores = []
    for t in range(1, STEPS):
        now, old = halves[t % 2], halves[1 - t % 2]

        @pl.loop(0, thick_blocks)
        def _(i):
            local_part(now, old, t, i * THICK)

        @pl.loop(edge_blocks, blocks - edge_blocks)
        def _(i):
            side_part(now, old, i * PLANES, every[1:-1])

        wait_x(now)
        wait_y(now)

        @pl.loop(0, 2 * edge_blocks)
        def _(i):
            block = i + (i // edge_blocks) * (blocks - 2 * edge_blocks)
            side_part(now, old, block * PLANES, every)

        if t + 1 < STEPS:
            send_x(old)

        for part in range(2):

            @pl.loop((edge_blocks, blocks // 2)[part], (blocks // 2, blocks - edge_blocks)[part])
            def _(i):
                side_part(now, old, i * PLANES, (every[0], every[-1]))

            if t + 2 >= STEPS:
                out = (before_ref, after_ref)[t + 2 - STEPS]
                half_x = size_x // 2
                for k in range(tiles):
                    stores.append(
                        pltpu.make_async_copy(
                            old.at[pl.ds(EDGE + part * half_x, half_x), k, inner, :],
                            out.at[pl.ds(part * half_x, half_x), :, pl.ds(k * LANES, LANES)],
                            store_sem.at[len(stores)],
                        )
                    )
                    stores[-1].start()

        if t + 1 < STEPS:
            send_y(old)
    for copy in stores:
        copy.wait()


def on_device(wave_prev, wave_now, courant, traces, pair_owner, pair_cell, green_tiles):
    slab_count, block_count = lax.axis_size("gx"), lax.axis_size("gy")
    owners = slab_count * block_count
    row_count = traces.shape[0]
    size_x, size_y, size_z = wave_now.shape
    tiles = size_z // LANES
    sent, sent_cells = pack(
        pair_owner.reshape(row_count // LANES, LANES),
        pair_cell.reshape(row_count // LANES, LANES),
        traces,
        owners,
    )
    hbm = pl.BlockSpec(memory_space=pltpu.HBM)
    vmem = pl.BlockSpec(memory_space=pltpu.VMEM)
    padded = (size_x + 2 * EDGE, tiles, size_y + 4 * EDGE, LANES)
    face = (2, size_x // 2, tiles, 2 * EDGE, LANES)
    return pl.pallas_call(
        wave_kernel,
        out_shape=[jax.ShapeDtypeStruct(wave_now.shape, F32)] * 2,
        in_specs=[hbm, hbm, hbm, vmem, vmem, hbm],
        out_specs=[vmem, hbm],
        scratch_shapes=[
            pltpu.VMEM(padded, F32),
            pltpu.VMEM(padded, F32),
            pltpu.VMEM((size_x, tiles, size_y, LANES), F32),
            pltpu.VMEM((owners, SLOTS, LANES), BF16),
            pltpu.VMEM((owners, 1, LANES), F32),
            pltpu.VMEM((slab_count, size_x * size_y, LANES), BF16),
            pltpu.VMEM(green_tiles.shape, BF16),
            pltpu.VMEM((STEPS - 1, size_x, tiles, size_y, LANES), F32),
            pltpu.VMEM((size_z, size_z), BF16),
            pltpu.VMEM(face, F32),
            pltpu.VMEM((2, *face), F32),
            pltpu.SemaphoreType.DMA((3 * tiles + 1,)),
            pltpu.SemaphoreType.DMA((4 * tiles,)),
            pltpu.SemaphoreType.DMA((4,)),
            pltpu.SemaphoreType.DMA((2, 4)),
            pltpu.SemaphoreType.DMA,
            pltpu.SemaphoreType.DMA((slab_count,)),
            pltpu.SemaphoreType.DMA,
            pltpu.SemaphoreType.DMA((slab_count,)),
        ],
        compiler_params=pltpu.CompilerParams(
            vmem_limit_bytes=43 << 20, collective_id=0, has_side_effects=True
        ),
    )(wave_prev, wave_now, courant, sent, sent_cells, green_tiles)


def solution(mesh):
    return jax.shard_map(
        on_device,
        mesh=mesh,
        in_specs=(
            P("gx", "gy", None),
            P("gx", "gy", None),
            P("gx", "gy", None),
            P(("gx", "gy"), None),
            P(("gx", "gy"), None),
            P(("gx", "gy")),
            P(("gx", "gy"), None),
        ),
        out_specs=(P("gx", "gy", None), P("gx", "gy", None)),
        check_vma=False,
    )
```

```python
import jax
import jax.numpy as jnp
from jax import lax
from jax.experimental import pallas as pl
from jax.experimental.pallas import tpu as pltpu
from jax.sharding import PartitionSpec as P

STEPS = 4
MESH = pl.DeviceIdType.MESH
F32 = jnp.float32
BF16 = jnp.bfloat16
LANES = 128
SLOTS = 64
EDGE = 4
PLANES = 2
THICK = 8

CENTER5 = 3.0 * -205.0 / 72.0 * 5.0
SIDE5 = (8.0, -1.0, 8.0 / 63.0, -1.0 / 112.0)


def iota(shape, dim):
    return lax.broadcasted_iota(jnp.int32, shape, dim)


def pack_kernel(
    owner_hbm, cell_hbm, trace_hbm, out_ref, out_cells,
    owner_ref, cell_ref, trace_ref, wide, rows32, slots_v, slots_s, cells_v, sem, load_sem,
):
    loads = [
        pltpu.make_async_copy(source, target, load_sem.at[i])
        for i, (source, target) in enumerate(
            ((owner_hbm, owner_ref), (cell_hbm, cell_ref), (trace_hbm, trace_ref))
        )
    ]
    for load in loads:
        load.start()
    blocks = owner_ref.shape[0]
    owners = out_ref.shape[0]
    before = (iota((LANES, 2 * LANES), 0) < iota((LANES, 2 * LANES), 1)).astype(F32).astype(BF16)
    carry = jnp.zeros((owners, LANES), F32)
    loads[0].wait()
    loads[1].wait()
    cells = jnp.zeros((owners, 2 * SLOTS), F32)
    for i in range(blocks):
        own = owner_ref[i : i + 1, :]
        cell = cell_ref[i : i + 1, :]
        hot = (own == iota((owners, LANES), 0)).astype(F32)
        hot16 = hot.astype(BF16)
        seen = jnp.dot(hot16, before, preferred_element_type=F32)
        rank = jnp.sum(hot * (seen[:, :LANES] + carry), axis=0, keepdims=True)
        carry = carry + seen[:, LANES:]
        rank = rank.astype(jnp.int32)
        slots_v[i : i + 1, :] = own * SLOTS + rank
        high = ((cell // SLOTS) + 1).astype(F32)
        low = (cell % SLOTS).astype(F32)
        place = iota((2 * SLOTS, LANES), 0)
        digit = jnp.where(place < SLOTS, high, low)
        digit = jnp.where(place % SLOTS == rank, digit, 0.0).astype(BF16)
        cells = cells + lax.dot_general(
            hot16, digit, (((1,), (1,)), ((), ())), preferred_element_type=F32
        )
    cells_v[...] = cells
    copy = pltpu.make_async_copy(slots_v, slots_s, sem)
    copy.start()

    @pl.loop(0, owners)
    def _(o):
        at = pl.multiple_of(o * SLOTS, SLOTS)
        wide[pl.ds(at, SLOTS), :] = jnp.zeros((SLOTS, LANES), F32)

    loads[2].wait()
    rows32[...] = trace_ref[...].astype(F32)
    copy.wait()

    @pl.loop(0, blocks)
    def _(i):
        base = pl.multiple_of(i * LANES, LANES)
        for j in range(LANES):
            wide[pl.ds(slots_s[i, j], 1), :] = rows32[pl.ds(base + j, 1), :]

    @pl.loop(0, owners)
    def _(o):
        at = pl.multiple_of(o * SLOTS, SLOTS)
        out_ref[o] = wide[pl.ds(at, SLOTS), :].astype(BF16)
        out_cells[o] = cells_v[pl.ds(o, 1), :]


def pack(owner, cell, traces, owners):
    rows = traces.shape[0]
    blocks = rows // LANES
    vmem = pl.BlockSpec(memory_space=pltpu.VMEM)
    return pl.pallas_call(
        pack_kernel,
        out_shape=(
            jax.ShapeDtypeStruct((owners, SLOTS, LANES), BF16),
            jax.ShapeDtypeStruct((owners, 1, LANES), F32),
        ),
        in_specs=[pl.BlockSpec(memory_space=pltpu.HBM)] * 3,
        out_specs=(vmem, vmem),
        scratch_shapes=[
            pltpu.VMEM((blocks, LANES), jnp.int32),
            pltpu.VMEM((blocks, LANES), jnp.int32),
            pltpu.VMEM((rows, LANES), BF16),
            pltpu.VMEM((owners * SLOTS, LANES), F32),
            pltpu.VMEM((rows, LANES), F32),
            pltpu.VMEM((blocks, LANES), jnp.int32),
            pltpu.SMEM((blocks, LANES), jnp.int32),
            pltpu.VMEM((owners, 2 * SLOTS), F32),
            pltpu.SemaphoreType.DMA,
            pltpu.SemaphoreType.DMA((3,)),
        ],
        compiler_params=pltpu.CompilerParams(vmem_limit_bytes=32 << 20),
    )(owner, cell, traces)


def sum_slab(rows, cells, gath, g, to, sources):
    cell_count = gath.shape[1]
    lane = iota((1, LANES), 1)
    highs, spots, values = [], [], []
    for i in range(0, sources, 2):
        one = cells[g * sources + i]
        two = cells[g * sources + i + 1]
        high = jnp.where(lane < SLOTS, one, pltpu.roll(two, SLOTS, 1))
        low = jnp.where(lane < SLOTS, pltpu.roll(one, SLOTS, 1), two)
        highs.append(high)
        spots.append((iota((SLOTS, LANES), 0).astype(F32) == low).astype(F32).astype(BF16))
        values.append(rows[g * sources + i])
        values.append(rows[g * sources + i + 1])
    high = jnp.concatenate(highs, axis=1)
    spot = jnp.concatenate(spots, axis=1)
    value = jnp.concatenate(values, axis=0)
    part = 8
    for first in range(0, cell_count // SLOTS, part):
        picked = []
        for h in range(first, first + part):
            here = (high == float(h + 1)).astype(F32).astype(BF16)
            picked.append(spot * jnp.broadcast_to(here, spot.shape))
        hot = jnp.concatenate(picked, axis=0)
        total = jnp.dot(hot, value, preferred_element_type=F32)
        gath[to, first * SLOTS : (first + part) * SLOTS, :] = total.astype(BF16)


def wave_kernel(
    prev_ref, now_ref, courant_ref, sent, sent_cells, green_ref, before_ref, after_ref,
    first, second, speed, rows, cells, gath, green, later, band, ysend, yrecv,
    load_sem, store_sem, send_sem, recv_sem, row_send_sem, row_recv_sem, cell_send_sem, cell_recv_sem,
):
    gx, gy = lax.axis_index("gx"), lax.axis_index("gy")
    nx, ny = lax.axis_size("gx"), lax.axis_size("gy")
    size_x, size_y, size_z = now_ref.shape
    tiles = size_z // LANES
    slabs = gath.shape[0]
    halves = (first, second)
    low_y = 2 * EDGE
    inner = pl.ds(low_y, size_y)
    near = (
        (gx > 0, (lax.rem(gx + nx - 1, nx), gy)),
        (gx < nx - 1, (lax.rem(gx + 1, nx), gy)),
        (gy > 0, (gx, lax.rem(gy + ny - 1, ny))),
        (gy < ny - 1, (gx, lax.rem(gy + 1, ny))),
    )

    chips, depth = nx // 2, 4

    def there_x(along, core):
        return 2 * lax.rem(gx // 2 + along, chips) + lax.rem(gx + core, 2)

    there_zs = [lax.rem(lax.rem(gy, depth) + along, depth) for along in range(depth)]

    def there_y(step, along):
        return depth * lax.rem(gy // depth + step + along, ny // depth) + there_zs[along]

    barrier = pltpu.get_barrier_semaphore()

    @pl.loop(0, ny // depth)
    def _(step):
        for along in range(depth):
            y = there_y(step, along)
            for along_x in range(chips):
                for core in range(2):
                    device = (there_x(along_x, core), y)

                    def greet(device=device):
                        pl.semaphore_signal(barrier, inc=1, device_id=device, device_id_type=MESH)

                    if along == along_x == core == 0:
                        pl.when(step > 0)(greet)
                    else:
                        greet()

    loads = []
    for i, (source, target) in enumerate(((now_ref, first), (prev_ref, second))):
        for k in range(tiles):
            loads.append(
                pltpu.make_async_copy(
                    source.at[:, :, pl.ds(k * LANES, LANES)],
                    target.at[pl.ds(EDGE, size_x), k, inner, :],
                    load_sem.at[i * tiles + k],
                )
            )
    for k in range(tiles):
        loads.append(
            pltpu.make_async_copy(
                courant_ref.at[:, :, pl.ds(k * LANES, LANES)], speed.at[:, k], load_sem.at[2 * tiles + k]
            )
        )
    loads.append(pltpu.make_async_copy(green_ref, green, load_sem.at[3 * tiles]))
    for copy in loads:
        copy.start()

    for side in range(2):
        planes = (0, size_x + EDGE)[side]
        rows_at = (low_y - EDGE, low_y + size_y)[side]

        @pl.when(jnp.logical_not(near[side][0]))
        def _(planes=planes):
            for half in halves:
                for k in range(tiles):
                    half[planes : planes + EDGE, k, inner, :] = jnp.zeros((EDGE, size_y, LANES), F32)

        @pl.when(jnp.logical_not(near[2 + side][0]))
        def _(rows_at=rows_at):
            for half in halves:

                @pl.loop(EDGE, size_x + EDGE)
                def _(x, half=half):
                    half[x, :, rows_at : rows_at + EDGE, :] = jnp.zeros((tiles, EDGE, LANES), F32)

    shape = (size_z, size_z)
    apart = jnp.abs(iota(shape, 0) - iota(shape, 1))
    weight = jnp.zeros(shape, F32)
    for k in range(1, 5):
        weight = jnp.where(apart == k, SIDE5[k - 1], weight)
    band[...] = weight.astype(BF16)

    pl.semaphore_wait(barrier, nx * ny - 1)

    me = gx * ny + gy
    keep = (
        pltpu.make_async_copy(sent.at[me], rows.at[me], row_recv_sem.at[gx]),
        pltpu.make_async_copy(sent_cells.at[me], cells.at[me], cell_recv_sem.at[gx]),
    )

    def send_rows(along_x, core):
        own = isinstance(along_x, int) and along_x == core == 0

        @pl.loop(0, ny // depth)
        def _(step):
            for along in range(depth):
                y = there_y(step, along)

                def send(x=there_x(along_x, core), y=y):
                    there = x * ny + y
                    for source, target, out_sem, in_sem in (
                        (sent_cells, cells, cell_send_sem, cell_recv_sem),
                        (sent, rows, row_send_sem, row_recv_sem),
                    ):
                        pltpu.make_async_remote_copy(
                            src_ref=source.at[there],
                            dst_ref=target.at[me],
                            send_sem=out_sem,
                            recv_sem=in_sem.at[gx],
                            device_id=(x, y),
                            device_id_type=MESH,
                        ).start()

                if along == 0 and own:
                    pl.when(step > 0)(send)

                    @pl.when(step == 0)
                    def _():
                        for copy in keep:
                            copy.start()

                else:
                    send()

    def slab_of(turn):
        chip = lax.rem(gx // 2 + turn // 4 + lax.rem(turn, 2) * (chips // 2), chips)
        return 2 * chip + lax.rem(gx + turn // 2, 2)

    def wait_slab(turn):
        g = slab_of(turn)
        for target, in_sem in ((cells, cell_recv_sem), (rows, row_recv_sem)):
            part = target.at[pl.ds(g * ny, ny)]
            pltpu.make_async_copy(part, part, in_sem.at[g]).wait()

    def x_copy(half, side):
        source = EDGE if side == 0 else size_x
        target = size_x + EDGE if side == 0 else 0
        return pltpu.make_async_remote_copy(
            src_ref=half.at[pl.ds(source, EDGE), :, inner, :],
            dst_ref=half.at[pl.ds(target, EDGE), :, inner, :],
            send_sem=send_sem.at[side],
            recv_sem=recv_sem.at[int(half is second), 1 - side],
            device_id=near[side][1],
            device_id_type=MESH,
        )

    def y_copy(half, side):
        return pltpu.make_async_remote_copy(
            src_ref=ysend.at[side],
            dst_ref=yrecv.at[int(half is second), 1 - side],
            send_sem=send_sem.at[2 + side],
            recv_sem=recv_sem.at[int(half is second), 3 - side],
            device_id=near[2 + side][1],
            device_id_type=MESH,
        )

    def send_x(half):
        for side in range(2):

            @pl.when(near[side][0])
            def _(side=side):
                x_copy(half, side).start()

    def send_y(half):
        @pl.loop(0, size_x // 2)
        def _(i):
            for k in range(tiles):
                for j in range(2):
                    at = EDGE + 2 * i + j
                    to = pl.ds(EDGE * j, EDGE)
                    ysend[0, i, k, to, :] = half[at, k, low_y : low_y + EDGE, :]
                    ysend[1, i, k, to, :] = half[at, k, low_y + size_y - EDGE : low_y + size_y, :]

        for side in range(2):

            @pl.when(near[2 + side][0])
            def _(side=side):
                y_copy(half, side).start()

    def wait_x(half):
        for side in range(2):

            @pl.when(near[side][0])
            def _(side=side):
                x_copy(half, side).wait_send()
                x_copy(half, 1 - side).wait_recv()

    def wait_y(half):
        for side in range(2):

            @pl.when(near[2 + side][0])
            def _(side=side):
                y_copy(half, side).wait_send()
                y_copy(half, 1 - side).wait_recv()

                @pl.loop(0, size_x // 2)
                def _(i):
                    for k in range(tiles):
                        for j in range(2):
                            to = low_y - EDGE if side == 0 else low_y + size_y
                            half[EDGE + 2 * i + j, k, to : to + EDGE, :] = yrecv[
                                int(half is second), side, i, k, pl.ds(EDGE * j, EDGE), :
                            ]

    def source_of(half, t, base):
        at = pl.multiple_of(base * size_y, THICK * size_y)
        left, right = [], []
        for turn in range(half * slabs // 2, (half + 1) * slabs // 2):
            left.append(gath[turn, pl.ds(at, THICK * size_y), :])
            row = pl.multiple_of(slab_of(turn) * LANES, LANES)
            right.append(green[pl.ds(row, LANES), t * size_z : (t + 1) * size_z])
        return jnp.dot(
            jnp.concatenate(left, axis=1), jnp.concatenate(right, axis=0), preferred_element_type=F32
        )

    def local_part(now, old, t, base):
        count = THICK * size_y
        place = pl.ds(EDGE + base, THICK)
        flat = jnp.concatenate([now[place, k, inner, :].reshape(count, LANES) for k in range(tiles)], axis=1)
        top = flat.astype(BF16)
        rest = (flat - top.astype(F32)).astype(BF16)
        lap = jnp.dot(top, band[...], preferred_element_type=F32)
        lap = lap + jnp.dot(rest, band[...], preferred_element_type=F32)
        source = source_of(1, t, base) if t else None
        for k in range(tiles):
            lanes = slice(k * LANES, (k + 1) * LANES)
            here = flat[:, lanes]
            value = speed[pl.ds(base, THICK), k].reshape(count, LANES) * (CENTER5 * here + lap[:, lanes])
            value = value + (here + here) - old[place, k, inner, :].reshape(count, LANES)
            if t:
                value = value + source[:, lanes] + later[t - 1, pl.ds(base, THICK), k].reshape(count, LANES)
            old[place, k, inner, :] = value.reshape(THICK, size_y, LANES)

    def add_source(half, t, base):
        source = source_of(half, t, base)
        for k in range(tiles):
            lanes = source[:, k * LANES : (k + 1) * LANES].reshape(THICK, size_y, LANES)
            if t:
                later[t - 1, pl.ds(base, THICK), k] = lanes
            else:
                spot = (pl.ds(EDGE + base, THICK), k, inner, slice(None))
                second[spot] = second[spot] + lanes

    def side_part(now, old, base, ys):
        for k in range(tiles):
            for y in ys:
                column = [now[base + x, k, pl.ds(low_y + y, 8), :] for x in range(PLANES + 2 * EDGE)]
                for x in range(PLANES):
                    lap = None
                    for d in range(1, EDGE + 1):
                        beside = now[base + x + EDGE, k, pl.ds(low_y + y + d, 8), :]
                        beside = beside + now[base + x + EDGE, k, pl.ds(low_y + y - d, 8), :]
                        beside = beside + (column[x + EDGE + d] + column[x + EDGE - d])
                        if SIDE5[d - 1] == -1.0:
                            lap = lap - beside
                        else:
                            beside = SIDE5[d - 1] * beside
                            lap = beside if lap is None else lap + beside
                    spot = (base + x + EDGE, k, pl.ds(low_y + y, 8), slice(None))
                    old[spot] = old[spot] + speed[base + x, k, pl.ds(y, 8), :] * lap

    blocks = size_x // PLANES
    thick_blocks = size_x // THICK
    edge_blocks = EDGE // PLANES
    every = tuple(range(0, size_y, 8))

    send_rows(0, 0)
    send_rows(2, 0)
    for copy in loads[:tiles]:
        copy.wait()
    send_x(first)
    send_y(first)
    for copy in loads[tiles : 3 * tiles]:
        copy.wait()

    @pl.loop(0, size_x)
    def _(x):
        speed[x] = 0.2 * speed[x]

    @pl.loop(0, thick_blocks)
    def _(i):
        local_part(first, second, 0, i * THICK)

    send_rows(0, 1)
    send_rows(2, 1)
    wait_x(first)
    wait_y(first)

    @pl.loop(0, blocks)
    def _(i):
        side_part(first, second, i * PLANES, every)

    @pl.loop(0, slabs // 2)
    def _(turn):
        wait_slab(turn)
        send_rows(1 + lax.rem(turn, 2) * (chips // 2), turn // 2)
        sum_slab(rows, cells, gath, slab_of(turn), turn, ny)

    loads[3 * tiles].wait()
    for t in range(STEPS):

        @pl.loop(0, thick_blocks)
        def _(i, t=t):
            add_source(0, t, i * THICK)

    @pl.loop(slabs // 2, slabs)
    def _(turn):
        wait_slab(turn)
        sum_slab(rows, cells, gath, slab_of(turn), turn, ny)

    for target, out_sem in ((cells, cell_send_sem), (rows, row_send_sem)):
        most = target.at[pl.ds(0, nx * ny - 1)]
        pltpu.make_async_copy(most, most, out_sem).wait()

    @pl.loop(0, thick_blocks)
    def _(i):
        add_source(1, 0, i * THICK)

    send_x(second)
    send_y(second)

    stores = []
    for t in range(1, STEPS):
        now, old = halves[t % 2], halves[1 - t % 2]

        @pl.loop(0, thick_blocks)
        def _(i):
            local_part(now, old, t, i * THICK)

        @pl.loop(edge_blocks, blocks - edge_blocks)
        def _(i):
            side_part(now, old, i * PLANES, every[1:-1])

        wait_x(now)
        wait_y(now)

        @pl.loop(0, 2 * edge_blocks)
        def _(i):
            block = i + (i // edge_blocks) * (blocks - 2 * edge_blocks)
            side_part(now, old, block * PLANES, every)

        if t + 1 < STEPS:
            send_x(old)

        for part in range(2):

            @pl.loop((edge_blocks, blocks // 2)[part], (blocks // 2, blocks - edge_blocks)[part])
            def _(i):
                side_part(now, old, i * PLANES, (every[0], every[-1]))

            if t + 2 >= STEPS:
                out = (before_ref, after_ref)[t + 2 - STEPS]
                half_x = size_x // 2
                for k in range(tiles):
                    stores.append(
                        pltpu.make_async_copy(
                            old.at[pl.ds(EDGE + part * half_x, half_x), k, inner, :],
                            out.at[pl.ds(part * half_x, half_x), :, pl.ds(k * LANES, LANES)],
                            store_sem.at[len(stores)],
                        )
                    )
                    stores[-1].start()

        if t + 1 < STEPS:
            send_y(old)
    for copy in stores:
        copy.wait()


def on_device(wave_prev, wave_now, courant, traces, pair_owner, pair_cell, green_tiles):
    slab_count, block_count = lax.axis_size("gx"), lax.axis_size("gy")
    owners = slab_count * block_count
    row_count = traces.shape[0]
    size_x, size_y, size_z = wave_now.shape
    tiles = size_z // LANES
    sent, sent_cells = pack(
        pair_owner.reshape(row_count // LANES, LANES),
        pair_cell.reshape(row_count // LANES, LANES),
        traces,
        owners,
    )
    hbm = pl.BlockSpec(memory_space=pltpu.HBM)
    vmem = pl.BlockSpec(memory_space=pltpu.VMEM)
    padded = (size_x + 2 * EDGE, tiles, size_y + 4 * EDGE, LANES)
    face = (2, size_x // 2, tiles, 2 * EDGE, LANES)
    return pl.pallas_call(
        wave_kernel,
        out_shape=[jax.ShapeDtypeStruct(wave_now.shape, F32)] * 2,
        in_specs=[hbm, hbm, hbm, vmem, vmem, hbm],
        out_specs=[vmem, hbm],
        scratch_shapes=[
            pltpu.VMEM(padded, F32),
            pltpu.VMEM(padded, F32),
            pltpu.VMEM((size_x, tiles, size_y, LANES), F32),
            pltpu.VMEM((owners, SLOTS, LANES), BF16),
            pltpu.VMEM((owners, 1, LANES), F32),
            pltpu.VMEM((slab_count, size_x * size_y, LANES), BF16),
            pltpu.VMEM(green_tiles.shape, BF16),
            pltpu.VMEM((STEPS - 1, size_x, tiles, size_y, LANES), F32),
            pltpu.VMEM((size_z, size_z), BF16),
            pltpu.VMEM(face, F32),
            pltpu.VMEM((2, *face), F32),
            pltpu.SemaphoreType.DMA((3 * tiles + 1,)),
            pltpu.SemaphoreType.DMA((4 * tiles,)),
            pltpu.SemaphoreType.DMA((4,)),
            pltpu.SemaphoreType.DMA((2, 4)),
            pltpu.SemaphoreType.DMA,
            pltpu.SemaphoreType.DMA((slab_count,)),
            pltpu.SemaphoreType.DMA,
            pltpu.SemaphoreType.DMA((slab_count,)),
        ],
        compiler_params=pltpu.CompilerParams(
            vmem_limit_bytes=43 << 20, collective_id=0, has_side_effects=True
        ),
    )(wave_prev, wave_now, courant, sent, sent_cells, green_tiles)


def solution(mesh):
    return jax.shard_map(
        on_device,
        mesh=mesh,
        in_specs=(
            P("gx", "gy", None),
            P("gx", "gy", None),
            P("gx", "gy", None),
            P(("gx", "gy"), None),
            P(("gx", "gy"), None),
            P(("gx", "gy")),
            P(("gx", "gy"), None),
        ),
        out_specs=(P("gx", "gy", None), P("gx", "gy", None)),
        check_vma=False,
    )
```
